32 devices in a mesh: ob: 8 (over z, core), pt: 4 (over y, x).
Axes of the slice: x: 2, y: 2, z: 4, core: 2. Of those that a mesh axis runs over, the one named last changes fastest.
Arguments:
- orbitals: float32 [128, 262144], P(('ob', 'pt')), may hold values from -32 to 32, as said below
- potential: float32 [262144], replicated, may hold values from 0 to 2
- cutoff: float32 [1], replicated, may hold values from 0.4 to 1
- eigvec: float32 [128, 128], replicated, may hold values from -3 to 3, as said below
Outputs:
- gram: float32 [128, 128], P(('ob', 'pt'))
- hamil_sub: float32 [128, 128], P(('ob', 'pt'))
- rotated: float32 [128, 262144], P(None, ('ob', 'pt'))
- residual: float32 [128, 262144], P(None, ('ob', 'pt'))
- ritz: float32 [128], replicated
The draws below stay inside these ranges and needn't reach their ends.
Inputs may be any that keep to these rules, and one draw needn't show every extreme that they name: `orbitals`: each orbital is a rough field whose scale differs from orbital to orbital and from region to region of the grid. `eigvec`: A full-rank matrix with a unit-sized diagonal and independent off-diagonal entries.
All inputs are finite; a program needn't handle non-finite values.
Results may differ from the reference program's by a relative error of at most 0.00027.
Values sent between devices are 32-bit elements; how exact they have to be, the bound alone decides.
A program may use at most 128 MiB of HBM per device.

```python
import jax
import jax.numpy as jnp
from jax import lax

G = 64
DEGREE = 12
ORB_DEV = 4
NORB = 128
NPTS = 262144


def draw_orbitals(key, part):
    key_base = jax.random.fold_in(key, 11)
    key_scale = jax.random.fold_in(key, 13)
    key_region = jax.random.fold_in(key, 14)
    points = lax.iota(jnp.int32, NPTS)
    x_coord = points // (G * G)
    y_coord = points // G % G
    z_coord = points % G
    block_id = x_coord * 8 // G * 64 + y_coord * 8 // G * 8 + z_coord * 8 // G
    base = jnp.clip(jax.random.normal(key_base, (NORB, NPTS), jnp.float32), -4.0, 4.0)
    region_table = jnp.exp(jax.random.uniform(key_region, (512,), jnp.float32, jnp.log(0.5), jnp.log(2.0)))
    orb_scale = jnp.exp(jax.random.uniform(key_scale, (NORB, 1), jnp.float32, jnp.log(0.4), jnp.log(4.0)))
    region = region_table[block_id][None, :]
    return jnp.clip(base * orb_scale * region, -32.0, 32.0)


def draw_eigvec(key, part):
    key_off = jax.random.fold_in(key, 21)
    off_diag = jnp.clip(jax.random.normal(key_off, (NORB, NORB), jnp.float32), -4.0, 4.0)
    return jnp.eye(NORB, dtype=jnp.float32) + 0.6 * off_diag / jnp.sqrt(jnp.float32(NORB))


def setup_inputs(seed: int = 0) -> dict:
    key_of = jax.random.split(jax.random.key(seed), 5)
    orbitals = draw_orbitals(jax.random.fold_in(key_of[4], 71), 0)
    potential = jnp.clip(jax.random.uniform(key_of[1], (NPTS,), jnp.float32, 0.0, 2.0), 0.0, 2.0)
    cutoff = jnp.clip(jax.random.uniform(key_of[2], (1,), jnp.float32, 0.4, 1.0), 0.4, 1.0)
    eigvec = draw_eigvec(jax.random.fold_in(key_of[4], 71), 0)
    return dict(orbitals=orbitals, potential=potential, cutoff=cutoff, eigvec=eigvec)


upper_bound = 8.0
quot_eps = 1e-6


def apply_ham(fields, potential):
    points = fields.shape[-1]
    plane_len = G * G
    x_pair = jnp.roll(fields, plane_len, axis=-1) + jnp.roll(fields, -plane_len, axis=-1)
    cube_view = fields.reshape(fields.shape[0], G, plane_len)
    y_pair = (jnp.roll(cube_view, G, axis=-1) + jnp.roll(cube_view, -G, axis=-1)).reshape(fields.shape)
    z_index = lax.broadcasted_iota(jnp.int32, (1, points), 1) % G
    z_lower = jnp.where(z_index == 0, jnp.roll(fields, 1 - G, axis=-1), jnp.roll(fields, 1, axis=-1))
    z_upper = jnp.where(z_index == G - 1, jnp.roll(fields, G - 1, axis=-1), jnp.roll(fields, -1, axis=-1))
    return -0.5 * (x_pair + y_pair + z_lower + z_upper - 6.0 * fields) + potential * fields


def chebyshev(fields, potential, cutoff):
    center = 0.5 * (upper_bound + cutoff[0])
    half_width = 0.5 * (upper_bound - cutoff[0])
    current = (apply_ham(fields, potential) - center * fields) / half_width

    def advance(turn_idx, carry):
        previous, present = carry
        following = 2.0 * (apply_ham(present, potential) - center * present) / half_width - previous
        return (present, following)

    previous, current = lax.fori_loop(0, DEGREE - 1, advance, (fields, current))
    return current, apply_ham(current, potential)


def reference(orbitals, potential, cutoff, eigvec):
    blocks = orbitals.reshape(-1, ORB_DEV, NPTS)
    filtered, applied = lax.map(lambda block: chebyshev(block, potential, cutoff), blocks)
    filtered = filtered.reshape(NORB, NPTS)
    applied = applied.reshape(NORB, NPTS)
    high = lax.Precision.HIGHEST
    gram = jnp.dot(filtered, filtered.T, precision=high) / NPTS
    hamil_sub = jnp.dot(filtered, applied.T, precision=high) / NPTS
    rotated = jnp.dot(eigvec.T, filtered, precision=high)
    rot_applied = jnp.dot(eigvec.T, applied, precision=high)
    numer = jnp.sum(eigvec * jnp.dot(hamil_sub, eigvec, precision=high), axis=0)
    denom = jnp.sum(eigvec * jnp.dot(gram, eigvec, precision=high), axis=0)
    ritz = numer / (denom + quot_eps)
    residual = rot_applied - ritz[:, None] * rotated
    return (gram, hamil_sub, rotated, residual, ritz)
```

```python
import functools

import jax
import jax.numpy as jnp
from jax import lax
from jax.experimental import pallas as pl
from jax.experimental.pallas import tpu as pltpu
from jax.sharding import PartitionSpec as P

G = 64
DEGREE = 12
LANES = 128
upper_bound = 8.0
quot_eps = 1e-06


def stencil_masks(shape):
    lane = lax.broadcasted_iota(jnp.int32, shape, 2)
    sub = lax.broadcasted_iota(jnp.int32, shape, 1)
    high_lane = lane >= G
    z_coord = lane % G
    low_sub = sub < 4
    return (
        high_lane & ~low_sub,
        ~high_lane & low_sub,
        z_coord == G - 1,
        z_coord == 0,
    )


def neighbour_sum(v, x_lower, x_upper, masks):
    m_up, m_down, m_last, m_first = masks
    w = pltpu.roll(v, G, 2)
    r = pltpu.roll(w, 4, 1)
    above = jnp.concatenate([r[1:], r[:1]], axis=0)
    below = jnp.concatenate([r[-1:], r[:-1]], axis=0)
    t = jnp.where(m_up, above, jnp.where(m_down, below, r))
    z_lower = pltpu.roll(jnp.where(m_last, w, v), 1, 2)
    z_upper = pltpu.roll(jnp.where(m_first, w, v), LANES - 1, 2)
    return (x_lower + x_upper) + (w + t) + (z_lower + z_upper)


def filter_kernel(cut_ref, pot_ref, orb_ref, filt_ref, appl_ref, coef_ref, sem):
    blocks = filt_ref.shape[0]
    plane = blocks // G
    cut = cut_ref[0]
    center = 0.5 * (upper_bound + cut)
    half_width = 0.5 * (upper_bound - cut)
    inv = 1.0 / half_width
    copy = pltpu.make_async_copy(orb_ref, filt_ref, sem)
    copy.start()

    def prep(x, c):
        rows = pl.ds(x * plane, plane)
        coef_ref[rows] = (2.0 * inv) * (pot_ref[rows] + (3.0 - center))
        return c

    lax.fori_loop(0, G, prep, 0)
    copy.wait()
    masks = stencil_masks((plane, 8, LANES))

    def sweep(cur, dst, kind):
        def body(x, c):
            here = pl.ds(x * plane, plane)
            down = pl.ds(jnp.where(x == 0, G - 1, x - 1) * plane, plane)
            up = pl.ds(jnp.where(x == G - 1, 0, x + 1) * plane, plane)
            v = cur[here]
            g = coef_ref[here] * v - inv * neighbour_sum(v, cur[down], cur[up], masks)
            if kind == 0:
                dst[here] = 0.5 * g
            elif kind == 1:
                dst[here] = g - dst[here]
            else:
                dst[here] = (0.5 * half_width) * g + center * v
            return c

        lax.fori_loop(0, G, body, 0)

    sweep(filt_ref, appl_ref, 0)

    def pair(j, c):
        sweep(appl_ref, filt_ref, 1)
        sweep(filt_ref, appl_ref, 1)
        return c

    lax.fori_loop(0, (DEGREE - 2) // 2, pair, 0)
    sweep(appl_ref, filt_ref, 1)
    sweep(filt_ref, appl_ref, 2)


def chebyshev(flat, pot, cutoff):
    vmem = pl.BlockSpec(memory_space=pltpu.VMEM)
    return pl.pallas_call(
        filter_kernel,
        out_shape=(
            jax.ShapeDtypeStruct(flat.shape, jnp.float32),
            jax.ShapeDtypeStruct(flat.shape, jnp.float32),
        ),
        in_specs=[
            pl.BlockSpec(memory_space=pltpu.SMEM),
            vmem,
            pl.BlockSpec(memory_space=pl.ANY),
        ],
        out_specs=(vmem, vmem),
        scratch_shapes=[pltpu.VMEM(flat.shape, jnp.float32), pltpu.SemaphoreType.DMA],
        compiler_params=pltpu.CompilerParams(vmem_limit_bytes=48 * 2**20),
        name="filter",
    )(cutoff, pot, flat)


def on_device(orbitals, potential, cutoff, eigvec):
    axes = ("ob", "pt")
    total_orb = eigvec.shape[0]
    n_dev = lax.axis_size("ob") * lax.axis_size("pt")
    per_dev, npts = orbitals.shape
    tiles = npts // LANES
    flat = orbitals.reshape(per_dev, tiles, LANES).transpose(1, 0, 2).reshape(-1, 8, LANES)
    pot = jnp.broadcast_to(
        potential.reshape(tiles, 1, LANES), (tiles, per_dev, LANES)
    ).reshape(-1, 8, LANES)
    filtered, applied = chebyshev(flat, pot, cutoff)

    def spread(a):
        a = a.reshape(n_dev, tiles // n_dev * per_dev, LANES)
        a = lax.all_to_all(a, axes, split_axis=0, concat_axis=0, tiled=True)
        a = a.reshape(n_dev, tiles // n_dev, per_dev, LANES)
        return a.transpose(0, 2, 1, 3).reshape(total_orb, npts // n_dev)

    filt, appl = spread(filtered), spread(applied)
    dot = functools.partial(jnp.dot, precision=lax.Precision.HIGH)
    part_gram = dot(filt, filt.T) / npts
    part_hamil = dot(filt, appl.T) / npts
    gram, hamil_sub = (
        lax.psum_scatter(part_gram, axes, scatter_dimension=0, tiled=True),
        lax.psum_scatter(part_hamil, axes, scatter_dimension=0, tiled=True),
    )
    rotated = dot(eigvec.T, filt)
    rot_applied = dot(eigvec.T, appl)
    numer = jnp.sum(rotated * rot_applied, axis=1) / npts
    denom = jnp.sum(rotated * rotated, axis=1) / npts
    numer, denom = lax.psum((numer, denom), axes)
    ritz = numer / (denom + quot_eps)
    residual = rot_applied - ritz[:, None] * rotated
    return (gram, hamil_sub, rotated, residual, ritz)


def solution(mesh):
    return jax.shard_map(
        on_device,
        mesh=mesh,
        in_specs=(P(("ob", "pt"), None), P(), P(), P()),
        out_specs=(
            P(("ob", "pt"), None),
            P(("ob", "pt"), None),
            P(None, ("ob", "pt")),
            P(None, ("ob", "pt")),
            P(),
        ),
        check_vma=False,
    )
```

```python
import functools

import jax
import jax.numpy as jnp
from jax import lax
from jax.experimental import pallas as pl
from jax.experimental.pallas import tpu as pltpu
from jax.sharding import PartitionSpec as P

G = 64
DEGREE = 12
LANES = 128
UNROLL = 16
MESH = pl.DeviceIdType.MESH
upper_bound = 8.0
quot_eps = 1e-06


def shift_matrix():
    row = lax.broadcasted_iota(jnp.int32, (2 * LANES, 2 * LANES), 0) % LANES
    col = lax.broadcasted_iota(jnp.int32, (2 * LANES, 2 * LANES), 1)
    lane = col % LANES
    step = (row - lane) % G
    z_pair = (row // G == lane // G) & ((step == 1) | (step == G - 1))
    swap = (row + G) % LANES == lane
    return jnp.where(col < LANES, z_pair, swap).astype(jnp.bfloat16)


def split(x):
    hi = x.astype(jnp.bfloat16)
    return hi, (x - hi.astype(jnp.float32)).astype(jnp.bfloat16)


def row_masks():
    shape = (1, 8, LANES)
    high_lane = lax.broadcasted_iota(jnp.int32, shape, 2) >= G
    low_sub = lax.broadcasted_iota(jnp.int32, shape, 1) < 4
    return high_lane & ~low_sub, ~high_lane & low_sub


def neighbour_sum(v, x_lower, x_upper, masks, shifts):
    m_up, m_down = masks
    hi, lo = split(v.reshape(-1, LANES))
    both = jnp.dot(
        jnp.concatenate([hi, lo], axis=1), shifts, preferred_element_type=jnp.float32
    )
    z_pair = both[:, :LANES].reshape(v.shape)
    w = both[:, LANES:].reshape(v.shape)
    r = pltpu.roll(w, 4, 1)
    above = jnp.concatenate([r[1:], r[:1]], axis=0)
    below = jnp.concatenate([r[-1:], r[:-1]], axis=0)
    t = jnp.where(m_up, above, jnp.where(m_down, below, r))
    return (x_lower + x_upper) + (w + t) + z_pair


def run_filter(cut_ref, pot_ref, orb_ref, shift_ref, filt, spare, coef_ref, sem):
    plane = pot_ref.shape[0] // G
    cut = cut_ref[0]
    center = 0.5 * (upper_bound + cut)
    half_width = 0.5 * (upper_bound - cut)
    inv = 1.0 / half_width
    copy = pltpu.make_async_copy(orb_ref, filt, sem)
    copy.start()

    def prep(x, c):
        rows = pl.ds(x * plane, plane)
        coef_ref[rows] = (2.0 * inv) * (pot_ref[rows] + (3.0 - center))
        return c

    lax.fori_loop(0, G, prep, 0)
    copy.wait()
    masks = row_masks()

    def sweep(cur, dst, first):
        def one(x):
            here = pl.ds(x * plane, plane)
            down = pl.ds((x + G - 1) % G * plane, plane)
            up = pl.ds((x + 1) % G * plane, plane)
            v = cur[here]
            s = neighbour_sum(v, cur[down], cur[up], masks, shift_ref[...])
            g = coef_ref[here] * v - inv * s
            return here, 0.5 * g if first else g - dst[here]

        def body(i, c):
            for here, value in [one(i * UNROLL + u) for u in range(UNROLL)]:
                dst[here] = value
            return c

        lax.fori_loop(0, G // UNROLL, body, 0)

    sweep(filt, spare, True)

    def pair(j, c):
        sweep(spare, filt, False)
        sweep(filt, spare, False)
        return c

    lax.fori_loop(0, (DEGREE - 2) // 2, pair, 0)
    sweep(spare, filt, False)


def filter_kernel(cut_ref, pot_ref, orb_ref, shift_ref, filt_ref, appl_ref, coef_ref, sem):
    run_filter(cut_ref, pot_ref, orb_ref, shift_ref, filt_ref, appl_ref, coef_ref, sem)
    plane = pot_ref.shape[0] // G
    masks = row_masks()

    def body(i, c):
        for u in range(UNROLL):
            x = i * UNROLL + u
            here = pl.ds(x * plane, plane)
            down = pl.ds((x + G - 1) % G * plane, plane)
            up = pl.ds((x + 1) % G * plane, plane)
            v = filt_ref[here]
            s = neighbour_sum(v, filt_ref[down], filt_ref[up], masks, shift_ref[...])
            appl_ref[here] = (pot_ref[here] + 3.0) * v - 0.5 * s
        return c

    lax.fori_loop(0, G // UNROLL, body, 0)


def chebyshev(flat, pot, cutoff):
    vmem = pl.BlockSpec(memory_space=pltpu.VMEM)
    return pl.pallas_call(
        filter_kernel,
        out_shape=(
            jax.ShapeDtypeStruct(flat.shape, jnp.float32),
            jax.ShapeDtypeStruct(flat.shape, jnp.float32),
        ),
        in_specs=[
            pl.BlockSpec(memory_space=pltpu.SMEM),
            vmem,
            pl.BlockSpec(memory_space=pl.ANY),
            vmem,
        ],
        out_specs=(vmem, vmem),
        scratch_shapes=[pltpu.VMEM(flat.shape, jnp.float32), pltpu.SemaphoreType.DMA],
        compiler_params=pltpu.CompilerParams(vmem_limit_bytes=48 * 2**20),
        name="filter",
    )(cutoff, pot, flat, shift_matrix())


def dot3(a, b, contract):
    dims = ((contract[:1], contract[1:]), ((), ()))
    one = functools.partial(
        lax.dot_general, dimension_numbers=dims, preferred_element_type=jnp.float32
    )
    return one(a[0], b[0]) + (one(a[0], b[1]) + one(a[1], b[0]))


def rotate_kernel(eig_ref, filt_ref, appl_ref, rot_ref, rota_ref, gram_ref, hamil_ref, num_ref, den_ref):
    rows = num_ref.shape[0]

    @pl.when(pl.program_id(0) == 0)
    def _():
        gram_ref[...] = jnp.zeros_like(gram_ref)
        hamil_ref[...] = jnp.zeros_like(hamil_ref)
        num_ref[...] = jnp.zeros_like(num_ref)
        den_ref[...] = jnp.zeros_like(den_ref)

    eig = split(eig_ref[...])

    def body(b, c):
        f = split(filt_ref[:, b].reshape(2 * rows, LANES))
        a = split(appl_ref[:, b].reshape(2 * rows, LANES))
        gram_ref[...] += dot3(f, f, (1, 1))
        hamil_ref[...] += dot3(f, a, (1, 1))
        rot = dot3(eig, f, (1, 0))
        rota = dot3(eig, a, (1, 0))
        for par in range(2):
            cols = pl.ds(pl.multiple_of((2 * b + par) * LANES, LANES), LANES)
            x = rot[par * rows : (par + 1) * rows]
            y = rota[par * rows : (par + 1) * rows]
            rot_ref[:, cols] = x
            rota_ref[:, cols] = y
            num_ref[...] += x * y
            den_ref[...] += x * x
        return c

    lax.fori_loop(0, filt_ref.shape[1], body, 0)


def rotate(filt, appl, eigvec):
    rows = eigvec.shape[0]
    n_src, blocks = filt.shape[:2]
    per_dev = rows // n_src
    step = min(blocks, max(1, 8 * 128 // rows))
    parity = lax.broadcasted_iota(jnp.int32, (2 * rows, 1), 0) // per_dev % 2
    doubled = jnp.broadcast_to(
        eigvec.reshape(n_src, 1, per_dev, rows), (n_src, 2, per_dev, rows)
    ).reshape(2 * rows, rows)
    spread = jnp.concatenate(
        [jnp.where(parity == 0, doubled, 0.0), jnp.where(parity == 1, doubled, 0.0)], axis=1
    ).T
    f32 = lambda *s: jax.ShapeDtypeStruct(s, jnp.float32)
    whole = lambda *s: pl.BlockSpec(s, lambda i: (0,) * len(s))
    field = pl.BlockSpec((n_src, step, 8, LANES), lambda i: (0, i, 0, 0))
    out = pl.BlockSpec((rows, 2 * step * LANES), lambda i: (0, i))
    rot, rota, gram, hamil, num, den = pl.pallas_call(
        rotate_kernel,
        grid=(blocks // step,),
        out_shape=(
            f32(rows, 2 * blocks * LANES),
            f32(rows, 2 * blocks * LANES),
            f32(2 * rows, 2 * rows),
            f32(2 * rows, 2 * rows),
            f32(rows, LANES),
            f32(rows, LANES),
        ),
        in_specs=[whole(2 * rows, 2 * rows), field, field],
        out_specs=(
            out,
            out,
            whole(2 * rows, 2 * rows),
            whole(2 * rows, 2 * rows),
            whole(rows, LANES),
            whole(rows, LANES),
        ),
        compiler_params=pltpu.CompilerParams(vmem_limit_bytes=56 * 2**20),
        name="rotate",
    )(spread, filt, appl)

    def fold(m):
        m = jnp.where(parity == parity.T, m, 0.0)
        half = m.reshape(n_src, 2, per_dev, 2 * rows).sum(axis=1).reshape(rows, 2 * rows).T
        return half.reshape(n_src, 2, per_dev, rows).sum(axis=1).reshape(rows, rows).T

    return rot, rota, fold(gram), fold(hamil), num.sum(axis=1), den.sum(axis=1)


def reduce_kernel(n_ob, n_pt, part_ref, out_ref, recv, send_sem, recv_sem):
    n_dev = n_ob * n_pt
    me = lax.axis_index("ob") * n_pt + lax.axis_index("pt")
    barrier = pltpu.get_barrier_semaphore()

    def copy(k):
        to = (me + k) % n_dev
        return pltpu.make_async_remote_copy(
            src_ref=part_ref.at[to],
            dst_ref=recv.at[k],
            send_sem=send_sem.at[k],
            recv_sem=recv_sem.at[k],
            device_id=(to // n_pt, to % n_pt),
            device_id_type=MESH,
        )

    def greet(k, c):
        to = (me + k) % n_dev
        pl.semaphore_signal(
            barrier, inc=1, device_id=(to // n_pt, to % n_pt), device_id_type=MESH
        )
        return c

    def start(k, c):
        copy(k).start()
        return c

    def finish(k, total):
        copy(k).wait()
        return total + recv[k]

    lax.fori_loop(1, n_dev, greet, 0)
    pl.semaphore_wait(barrier, n_dev - 1)
    lax.fori_loop(1, n_dev, start, 0)
    out_ref[...] = lax.fori_loop(1, n_dev, finish, part_ref[me])


def reduce_parts(parts, n_ob, n_pt):
    n_dev, rows, cols = parts.shape
    vmem = pl.BlockSpec(memory_space=pltpu.VMEM)
    return pl.pallas_call(
        functools.partial(reduce_kernel, n_ob, n_pt),
        out_shape=jax.ShapeDtypeStruct((rows, cols), jnp.float32),
        in_specs=[vmem],
        out_specs=vmem,
        scratch_shapes=[
            pltpu.VMEM((n_dev, rows, cols), jnp.float32),
            pltpu.SemaphoreType.DMA((n_dev,)),
            pltpu.SemaphoreType.DMA((n_dev,)),
        ],
        compiler_params=pltpu.CompilerParams(
            collective_id=1, has_side_effects=True, vmem_limit_bytes=32 * 2**20
        ),
        name="reduce_parts",
    )(parts)


def on_device(orbitals, potential, cutoff, eigvec):
    axes = ("ob", "pt")
    total_orb = eigvec.shape[0]
    n_ob, n_pt = lax.axis_size("ob"), lax.axis_size("pt")
    n_dev = n_ob * n_pt
    per_dev, npts = orbitals.shape
    tiles = npts // LANES
    flat = orbitals.reshape(per_dev, tiles, LANES).transpose(1, 0, 2).reshape(-1, 8, LANES)
    pot = jnp.broadcast_to(
        potential.reshape(tiles, 1, LANES), (tiles, per_dev, LANES)
    ).reshape(-1, 8, LANES)
    filtered, applied = chebyshev(flat, pot, cutoff)

    def spread(a):
        a = a.reshape(n_dev, -1, LANES)
        a = lax.all_to_all(a, axes, split_axis=0, concat_axis=0, tiled=True)
        return a.reshape(n_dev, -1, 8, LANES)

    rotated, rot_applied, gram, hamil, numer, denom = rotate(
        spread(filtered), spread(applied), eigvec
    )
    quotient = jnp.broadcast_to(jnp.stack([numer, denom]), (n_dev, 2, total_orb))
    parts = jnp.concatenate(
        [
            gram.reshape(n_dev, per_dev, total_orb),
            hamil.reshape(n_dev, per_dev, total_orb),
            quotient,
            jnp.zeros((n_dev, -(2 * per_dev + 2) % 8, total_orb), jnp.float32),
        ],
        axis=1,
    )
    sums = reduce_parts(parts, n_ob, n_pt) / npts
    gram, hamil_sub = sums[:per_dev], sums[per_dev : 2 * per_dev]
    numer, denom = sums[2 * per_dev], sums[2 * per_dev + 1]
    ritz = numer / (denom + quot_eps)
    residual = rot_applied - ritz[:, None] * rotated
    return (gram, hamil_sub, rotated, residual, ritz)


def solution(mesh):
    return jax.shard_map(
        on_device,
        mesh=mesh,
        in_specs=(P(("ob", "pt"), None), P(), P(), P()),
        out_specs=(
            P(("ob", "pt"), None),
            P(("ob", "pt"), None),
            P(None, ("ob", "pt")),
            P(None, ("ob", "pt")),
            P(),
        ),
        check_vma=False,
    )
```

```python
import functools

import jax
import jax.numpy as jnp
from jax import lax
from jax.experimental import pallas as pl
from jax.experimental.pallas import tpu as pltpu
from jax.sharding import PartitionSpec as P

G = 64
DEGREE = 12
LANES = 128
UNROLL = 16
MESH = pl.DeviceIdType.MESH
upper_bound = 8.0
quot_eps = 1e-06


def shift_matrix():
    row = lax.broadcasted_iota(jnp.int32, (2 * LANES, 2 * LANES), 0) % LANES
    col = lax.broadcasted_iota(jnp.int32, (2 * LANES, 2 * LANES), 1)
    lane = col % LANES
    step = (row - lane) % G
    z_pair = (row // G == lane // G) & ((step == 1) | (step == G - 1))
    swap = (row + G) % LANES == lane
    return jnp.where(col < LANES, z_pair, swap).astype(jnp.bfloat16)


def split(x):
    hi = x.astype(jnp.bfloat16)
    return hi, (x - hi.astype(jnp.float32)).astype(jnp.bfloat16)


def row_masks():
    shape = (1, 8, LANES)
    high_lane = lax.broadcasted_iota(jnp.int32, shape, 2) >= G
    low_sub = lax.broadcasted_iota(jnp.int32, shape, 1) < 4
    return high_lane & ~low_sub, ~high_lane & low_sub


def neighbour_sum(v, x_lower, x_upper, masks, shifts):
    m_up, m_down = masks
    hi, lo = split(v.reshape(-1, LANES))
    both = jnp.dot(
        jnp.concatenate([hi, lo], axis=1), shifts, preferred_element_type=jnp.float32
    )
    z_pair = both[:, :LANES].reshape(v.shape)
    w = both[:, LANES:].reshape(v.shape)
    r = pltpu.roll(w, 4, 1)
    above = jnp.concatenate([r[1:], r[:1]], axis=0)
    below = jnp.concatenate([r[-1:], r[:-1]], axis=0)
    t = jnp.where(m_up, above, jnp.where(m_down, below, r))
    return (x_lower + x_upper) + (w + t) + z_pair


def run_filter(cut_ref, pot_ref, orb_ref, shift_ref, filt, spare, coef_ref, sem):
    plane = pot_ref.shape[0] // G
    cut = cut_ref[0]
    center = 0.5 * (upper_bound + cut)
    half_width = 0.5 * (upper_bound - cut)
    inv = 1.0 / half_width
    copy = pltpu.make_async_copy(orb_ref, filt, sem)
    copy.start()

    def prep(x, c):
        rows = pl.ds(x * plane, plane)
        coef_ref[rows] = (2.0 * inv) * (pot_ref[rows] + (3.0 - center))
        return c

    lax.fori_loop(0, G, prep, 0)
    copy.wait()
    masks = row_masks()

    def sweep(cur, dst, first):
        def one(x):
            here = pl.ds(x * plane, plane)
            down = pl.ds((x + G - 1) % G * plane, plane)
            up = pl.ds((x + 1) % G * plane, plane)
            v = cur[here]
            s = neighbour_sum(v, cur[down], cur[up], masks, shift_ref[...])
            g = coef_ref[here] * v - inv * s
            return here, 0.5 * g if first else g - dst[here]

        def body(i, c):
            for here, value in [one(i * UNROLL + u) for u in range(UNROLL)]:
                dst[here] = value
            return c

        lax.fori_loop(0, G // UNROLL, body, 0)

    sweep(filt, spare, True)

    def pair(j, c):
        sweep(spare, filt, False)
        sweep(filt, spare, False)
        return c

    lax.fori_loop(0, (DEGREE - 2) // 2, pair, 0)
    sweep(spare, filt, False)


def filter_kernel(n_ob, n_pt, cut_ref, pot_ref, orb_ref, shift_ref, filt_out, appl_out, ext, spare, coef_ref, zbuf, sem, zsend, zrecv, psend, precv, own_sem):
    blocks = pot_ref.shape[0]
    plane = blocks // G
    outer = n_ob // 2
    peers = 2 * n_pt
    slab = blocks // outer
    piece = slab // peers
    ob, pt = lax.axis_index("ob"), lax.axis_index("pt")
    group = ob // 2
    seat = ob % 2 * n_pt + pt

    def group_dev(d):
        return ((group + d) % outer * 2 + ob % 2, pt)

    def peer_dev(k):
        to = (seat + k) % peers
        return (group * 2 + to // n_pt, to % n_pt)

    barrier = pltpu.get_barrier_semaphore()
    for d in range(1, outer):
        pl.semaphore_signal(barrier, inc=1, device_id=group_dev(d), device_id_type=MESH)
    for k in range(1, peers):
        pl.semaphore_signal(barrier, inc=1, device_id=peer_dev(k), device_id_type=MESH)

    filt = ext.at[pl.ds(plane, blocks)]
    run_filter(cut_ref, pot_ref, orb_ref, shift_ref, filt, spare, coef_ref, sem)
    ext[pl.ds(0, plane)] = ext[pl.ds(blocks, plane)]
    ext[pl.ds(plane + blocks, plane)] = ext[pl.ds(plane, plane)]
    pl.semaphore_wait(barrier, outer + peers - 2)

    def zcopy(d):
        return pltpu.make_async_remote_copy(
            src_ref=ext.at[pl.ds((group + d) % outer * slab, slab + 2 * plane)],
            dst_ref=zbuf.at[d - 1],
            send_sem=zsend.at[d],
            recv_sem=zrecv.at[d],
            device_id=group_dev(d),
            device_id_type=MESH,
        )

    for d in range(1, outer):
        zcopy(d).start()
    masks = row_masks()
    unroll = min(8, slab // plane)

    def source(d):
        return ext.at[pl.ds(group * slab, slab + 2 * plane)] if d == 0 else zbuf.at[d - 1]

    def pcopies(d, k):
        to = (seat + k) % peers
        slot = (group + outer - d) % outer * peers + seat
        srcs = (
            source(d).at[pl.ds(plane + to * piece, piece)],
            spare.at[pl.ds(d * slab + to * piece, piece)],
        )
        return [
            pltpu.make_async_remote_copy(
                src_ref=srcs[i],
                dst_ref=out.at[slot],
                send_sem=psend.at[d, k, i],
                recv_sem=precv.at[d, k, i],
                device_id=peer_dev(k),
                device_id_type=MESH,
            )
            for i, out in enumerate((filt_out, appl_out))
        ]

    def own_copies(d):
        slot = (group + outer - d) % outer * peers + seat
        srcs = (
            source(d).at[pl.ds(plane + seat * piece, piece)],
            spare.at[pl.ds(d * slab + seat * piece, piece)],
        )
        return [
            pltpu.make_async_copy(srcs[i], out.at[slot], own_sem.at[d, i])
            for i, out in enumerate((filt_out, appl_out))
        ]

    for d in range(outer):
        if d > 0:
            zcopy(d).wait_recv()
        src = source(d)

        def body(i, c):
            for u in range(unroll):
                x = i * unroll + u
                v = src[pl.ds((x + 1) * plane, plane)]
                s = neighbour_sum(
                    v,
                    src[pl.ds(x * plane, plane)],
                    src[pl.ds((x + 2) * plane, plane)],
                    masks,
                    shift_ref[...],
                )
                rows = pl.ds(group * slab + x * plane, plane)
                spare[pl.ds(d * slab + x * plane, plane)] = (pot_ref[rows] + 3.0) * v - 0.5 * s
            return c

        lax.fori_loop(0, slab // plane // unroll, body, 0)

        def send(k, c):
            for copy in pcopies(d, k):
                copy.start()
            return c

        lax.fori_loop(1, peers, send, 0)
        for copy in own_copies(d):
            copy.start()

    for d in range(outer):

        def finish(k, c):
            for copy in pcopies(d, k):
                copy.wait()
            return c

        lax.fori_loop(1, peers, finish, 0)
        for copy in own_copies(d):
            copy.wait()
        if d > 0:
            zcopy(d).wait_send()


def chebyshev(flat, pot, cutoff, n_ob, n_pt):
    vmem = pl.BlockSpec(memory_space=pltpu.VMEM)
    anywhere = pl.BlockSpec(memory_space=pl.ANY)
    blocks = flat.shape[0]
    outer, peers, plane = n_ob // 2, 2 * n_pt, blocks // G
    slab = blocks // outer
    result = jax.ShapeDtypeStruct((n_ob * n_pt, slab // peers, 8, LANES), jnp.float32)
    dma = pltpu.SemaphoreType.DMA
    return pl.pallas_call(
        functools.partial(filter_kernel, n_ob, n_pt),
        out_shape=(result, result),
        in_specs=[pl.BlockSpec(memory_space=pltpu.SMEM), vmem, anywhere, vmem],
        out_specs=(anywhere, anywhere),
        scratch_shapes=[
            pltpu.VMEM((blocks + 2 * plane, 8, LANES), jnp.float32),
            pltpu.VMEM(flat.shape, jnp.float32),
            pltpu.VMEM(flat.shape, jnp.float32),
            pltpu.VMEM((outer - 1, slab + 2 * plane, 8, LANES), jnp.float32),
            dma,
            dma((outer,)),
            dma((outer,)),
            dma((outer, peers, 2)),
            dma((outer, peers, 2)),
            dma((outer, 2)),
        ],
        compiler_params=pltpu.CompilerParams(
            collective_id=0, has_side_effects=True, vmem_limit_bytes=48 * 2**20
        ),
        name="filter",
    )(cutoff, pot, flat, shift_matrix())


def dot3(a, b, contract):
    dims = ((contract[:1], contract[1:]), ((), ()))
    one = functools.partial(
        lax.dot_general, dimension_numbers=dims, preferred_element_type=jnp.float32
    )
    return one(a[0], b[0]) + (one(a[0], b[1]) + one(a[1], b[0]))


def rotate_kernel(eig_ref, filt_ref, appl_ref, rot_ref, rota_ref, gram_ref, hamil_ref, num_ref, den_ref):
    rows = num_ref.shape[0]

    @pl.when(pl.program_id(0) == 0)
    def _():
        gram_ref[...] = jnp.zeros_like(gram_ref)
        hamil_ref[...] = jnp.zeros_like(hamil_ref)
        num_ref[...] = jnp.zeros_like(num_ref)
        den_ref[...] = jnp.zeros_like(den_ref)

    eig = split(eig_ref[...])

    def body(b, c):
        f = split(filt_ref[:, b].reshape(2 * rows, LANES))
        a = split(appl_ref[:, b].reshape(2 * rows, LANES))
        gram_ref[...] += dot3(f, f, (1, 1))
        hamil_ref[...] += dot3(f, a, (1, 1))
        rot = dot3(eig, f, (1, 0))
        rota = dot3(eig, a, (1, 0))
        for par in range(2):
            cols = pl.ds(pl.multiple_of((2 * b + par) * LANES, LANES), LANES)
            x = rot[par * rows : (par + 1) * rows]
            y = rota[par * rows : (par + 1) * rows]
            rot_ref[:, cols] = x
            rota_ref[:, cols] = y
            num_ref[...] += x * y
            den_ref[...] += x * x
        return c

    lax.fori_loop(0, filt_ref.shape[1], body, 0)


def rotate(filt, appl, eigvec):
    rows = eigvec.shape[0]
    n_src, blocks = filt.shape[:2]
    per_dev = rows // n_src
    step = min(blocks, max(1, 8 * 128 // rows))
    parity = lax.broadcasted_iota(jnp.int32, (2 * rows, 1), 0) // per_dev % 2
    doubled = jnp.broadcast_to(
        eigvec.reshape(n_src, 1, per_dev, rows), (n_src, 2, per_dev, rows)
    ).reshape(2 * rows, rows)
    spread = jnp.concatenate(
        [jnp.where(parity == 0, doubled, 0.0), jnp.where(parity == 1, doubled, 0.0)], axis=1
    ).T
    f32 = lambda *s: jax.ShapeDtypeStruct(s, jnp.float32)
    whole = lambda *s: pl.BlockSpec(s, lambda i: (0,) * len(s))
    field = pl.BlockSpec((n_src, step, 8, LANES), lambda i: (0, i, 0, 0))
    out = pl.BlockSpec((rows, 2 * step * LANES), lambda i: (0, i))
    rot, rota, gram, hamil, num, den = pl.pallas_call(
        rotate_kernel,
        grid=(blocks // step,),
        out_shape=(
            f32(rows, 2 * blocks * LANES),
            f32(rows, 2 * blocks * LANES),
            f32(2 * rows, 2 * rows),
            f32(2 * rows, 2 * rows),
            f32(rows, LANES),
            f32(rows, LANES),
        ),
        in_specs=[whole(2 * rows, 2 * rows), field, field],
        out_specs=(
            out,
            out,
            whole(2 * rows, 2 * rows),
            whole(2 * rows, 2 * rows),
            whole(rows, LANES),
            whole(rows, LANES),
        ),
        compiler_params=pltpu.CompilerParams(vmem_limit_bytes=56 * 2**20),
        name="rotate",
    )(spread, filt, appl)

    def fold(m):
        m = jnp.where(parity == parity.T, m, 0.0)
        half = m.reshape(n_src, 2, per_dev, 2 * rows).sum(axis=1).reshape(rows, 2 * rows).T
        return half.reshape(n_src, 2, per_dev, rows).sum(axis=1).reshape(rows, rows).T

    return rot, rota, fold(gram), fold(hamil), num.sum(axis=1), den.sum(axis=1)


def reduce_kernel(n_ob, n_pt, part_ref, out_ref, recv, send_sem, recv_sem):
    n_dev = n_ob * n_pt
    me = lax.axis_index("ob") * n_pt + lax.axis_index("pt")
    barrier = pltpu.get_barrier_semaphore()

    def copy(k):
        to = (me + k) % n_dev
        return pltpu.make_async_remote_copy(
            src_ref=part_ref.at[to],
            dst_ref=recv.at[k],
            send_sem=send_sem.at[k],
            recv_sem=recv_sem.at[k],
            device_id=(to // n_pt, to % n_pt),
            device_id_type=MESH,
        )

    def greet(k, c):
        to = (me + k) % n_dev
        pl.semaphore_signal(
            barrier, inc=1, device_id=(to // n_pt, to % n_pt), device_id_type=MESH
        )
        return c

    def start(k, c):
        copy(k).start()
        return c

    def finish(k, total):
        copy(k).wait()
        return total + recv[k]

    lax.fori_loop(1, n_dev, greet, 0)
    pl.semaphore_wait(barrier, n_dev - 1)
    lax.fori_loop(1, n_dev, start, 0)
    out_ref[...] = lax.fori_loop(1, n_dev, finish, part_ref[me])


def reduce_parts(parts, n_ob, n_pt):
    n_dev, rows, cols = parts.shape
    vmem = pl.BlockSpec(memory_space=pltpu.VMEM)
    return pl.pallas_call(
        functools.partial(reduce_kernel, n_ob, n_pt),
        out_shape=jax.ShapeDtypeStruct((rows, cols), jnp.float32),
        in_specs=[vmem],
        out_specs=vmem,
        scratch_shapes=[
            pltpu.VMEM((n_dev, rows, cols), jnp.float32),
            pltpu.SemaphoreType.DMA((n_dev,)),
            pltpu.SemaphoreType.DMA((n_dev,)),
        ],
        compiler_params=pltpu.CompilerParams(
            collective_id=1, has_side_effects=True, vmem_limit_bytes=32 * 2**20
        ),
        name="reduce_parts",
    )(parts)


def on_device(orbitals, potential, cutoff, eigvec):
    axes = ("ob", "pt")
    total_orb = eigvec.shape[0]
    n_ob, n_pt = lax.axis_size("ob"), lax.axis_size("pt")
    n_dev = n_ob * n_pt
    per_dev, npts = orbitals.shape
    tiles = npts // LANES
    flat = orbitals.reshape(per_dev, tiles, LANES).transpose(1, 0, 2).reshape(-1, 8, LANES)
    pot = jnp.broadcast_to(
        potential.reshape(tiles, 1, LANES), (tiles, per_dev, LANES)
    ).reshape(-1, 8, LANES)
    filtered, applied = chebyshev(flat, pot, cutoff, n_ob, n_pt)
    rotated, rot_applied, gram, hamil, numer, denom = rotate(filtered, applied, eigvec)
    quotient = jnp.broadcast_to(jnp.stack([numer, denom]), (n_dev, 2, total_orb))
    parts = jnp.concatenate(
        [
            gram.reshape(n_dev, per_dev, total_orb),
            hamil.reshape(n_dev, per_dev, total_orb),
            quotient,
            jnp.zeros((n_dev, -(2 * per_dev + 2) % 8, total_orb), jnp.float32),
        ],
        axis=1,
    )
    sums = reduce_parts(parts, n_ob, n_pt) / npts
    gram, hamil_sub = sums[:per_dev], sums[per_dev : 2 * per_dev]
    numer, denom = sums[2 * per_dev], sums[2 * per_dev + 1]
    ritz = numer / (denom + quot_eps)
    residual = rot_applied - ritz[:, None] * rotated
    return (gram, hamil_sub, rotated, residual, ritz)


def solution(mesh):
    return jax.shard_map(
        on_device,
        mesh=mesh,
        in_specs=(P(("ob", "pt"), None), P(), P(), P()),
        out_specs=(
            P(("ob", "pt"), None),
            P(("ob", "pt"), None),
            P(None, ("ob", "pt")),
            P(None, ("ob", "pt")),
            P(),
        ),
        check_vma=False,
    )
```
